128 devices in a mesh: outer: 8 (over z, core), inner: 16 (over x, y).
Axes of the slice: x: 4, y: 4, z: 4, core: 2. Of those that a mesh axis runs over, the one named last changes fastest.
Arguments:
- queries: bfloat16 [131072, 2048], P(('outer', 'inner')), may hold values from -6 to 6
- key_rows: bfloat16 [131072, 2048], P(('outer', 'inner')), may hold values from -6 to 6
- value_rows: bfloat16 [131072, 2048], P(('outer', 'inner')), may hold values from -6 to 6
- norm_gain: float32 [2048], replicated, may hold values from 0.5 to 1.5
Outputs:
- mixed: bfloat16 [131072, 2048], P(('outer', 'inner'))
- final_state: float32 [131072], P(('outer', 'inner'))
The draws below stay inside these ranges and needn't reach their ends.
All inputs are finite; a program needn't handle non-finite values.
Results may differ from the reference program's by a relative error of at most 0.005.
Values sent between devices are 32-bit elements; how exact they have to be, the bound alone decides.
No kernel may reach another device: no remote copies, remote signals or barrier semaphores. Data moves between devices by JAX's collectives and lax.ppermute only.
A program may use at most 256 MiB of HBM per device.

```python
import jax
import jax.numpy as jnp
from jax import lax

D = 2048
HEADS = 32
DK = 64
BLOCK = 128
TOKENS = 131072


def steps_of(stream_key, shape, split, low, largest):
    gain = 1.0
    for position, blocks in split:
        heights = jax.random.uniform(jax.random.fold_in(jax.random.fold_in(stream_key, 6), position), (blocks,), jnp.float32, low / len(split), largest / len(split))
        gain = gain * jnp.repeat(jnp.exp(heights), shape[position] // blocks).reshape((-1,) + (1,) * (len(shape) - 1 - position))
    return gain


def normal_values(rng, shape, spread, bound, cuts=(), dtype=jnp.bfloat16):
    array = jax.random.normal(rng, shape, jnp.float32) * spread
    if len(cuts) > 0:
        array = steps_of(rng, shape, cuts, -0.22, 0.18) * array
    return jnp.clip(array, min=-bound, max=bound).astype(dtype)


def setup_inputs(seed: int = 0) -> dict:
    splits = jax.random.split(jax.random.key(seed), 5)
    return {
        "queries": normal_values(splits[0], (TOKENS, D), 1.0, 6.0, ((0, 128),)),
        "key_rows": normal_values(splits[1], (TOKENS, D), 1.0, 6.0, ((0, 128),)),
        "value_rows": normal_values(splits[2], (TOKENS, D), 1.0, 6.0, ((0, 128),)),
        "norm_gain": jnp.clip(1.0 + 0.1 * jax.random.normal(splits[3], (D,), jnp.float32), 0.5, 1.5),
    }


def reference(queries, key_rows, value_rows, norm_gain):
    blocks = TOKENS // BLOCK
    query_grid = queries.reshape(blocks, BLOCK, HEADS, DK)
    key_grid = key_rows.reshape(blocks, BLOCK, HEADS, DK)
    value_grid = value_rows.reshape(blocks, BLOCK, HEADS, DK)
    causal = jnp.tril(jnp.ones((BLOCK, BLOCK), jnp.float32))
    gain_grid = norm_gain.reshape(HEADS, DK).astype(jnp.float32)

    def advance(carry_state, pieces):
        query_block, key_block, value_block = pieces
        query_wide = query_block.astype(jnp.float32)
        key_wide = key_block.astype(jnp.float32)
        value_wide = value_block.astype(jnp.float32)
        rounded = lax.optimization_barrier(carry_state.astype(jnp.bfloat16)).astype(jnp.float32)
        carried = jnp.einsum('qhd,hde->qhe', query_wide, rounded)
        scores = jnp.einsum('qhd,khd->hqk', query_wide, key_wide) * causal
        weights = lax.optimization_barrier(scores.astype(jnp.bfloat16)).astype(jnp.float32)
        inside = jnp.einsum('hqk,khe->qhe', weights, value_wide)
        attended = carried + inside
        scaled = attended * lax.rsqrt(lax.optimization_barrier(jnp.mean(attended * attended, axis=-1, keepdims=True)) + 1e-06) * gain_grid
        update = jnp.einsum('khd,khe->hde', key_wide, value_wide)
        return (carry_state + update, scaled.reshape(BLOCK, D).astype(jnp.bfloat16))
    start_state = jnp.zeros((HEADS, DK, DK), jnp.float32)
    last_state, mixed = lax.scan(advance, start_state, (query_grid, key_grid, value_grid))
    return (mixed.reshape(TOKENS, D), (last_state * float(TOKENS) ** (-0.5)).reshape(HEADS * DK * DK))
```

```python
import functools

import jax
import jax.numpy as jnp
from jax import lax
from jax.experimental import pallas as pl
from jax.experimental.pallas import tpu as pltpu
from jax.sharding import PartitionSpec as P


HEADS = 32
DK = 64
BLOCK = 128
LANES = 128
PAIRS = 16
ROWS = 1024
BLOCKS = ROWS // BLOCK
GROUPS = 4
GROUP_PAIRS = PAIRS // GROUPS
GROUP_COLS = GROUP_PAIRS * LANES
QUARTERS = 4
QROWS = DK // QUARTERS
AXES = ("outer", "inner")


def coordinates():
    outer, inner = lax.axis_index("outer"), lax.axis_index("inner")
    return outer // 2, outer % 2, inner // 4, inner % 4


def exchange(array, dz=0, dc=0, dx=0, dy=0):
    turn = ((dz * 2 + dc) * 4 + dx) * 4 + dy
    return lax.ppermute(array, AXES, [(rank, rank ^ turn) for rank in range(128)])


def on_chip(array):
    return pltpu.with_memory_space_constraint(array, pltpu.VMEM)


def off_chip(array):
    return pltpu.with_memory_space_constraint(array, pltpu.HBM)


def pair_state(key, value):
    full = lax.dot_general(
        key, value, (((0,), (0,)), ((), ())), preferred_element_type=jnp.float32
    )
    lane = lax.broadcasted_iota(jnp.int32, (DK, LANES), 1)
    return jnp.where(lane < DK, full[:DK], full[DK:])


def totals_kernel(k_hbm, v_hbm, total_ref, k_ref, v_ref, sems):
    copies = []
    for i in range(GROUPS):
        cols = pl.ds(i * GROUP_COLS, GROUP_COLS)
        pair = (
            pltpu.make_async_copy(k_hbm.at[:, cols], k_ref.at[:, cols], sems.at[0, i]),
            pltpu.make_async_copy(v_hbm.at[:, cols], v_ref.at[:, cols], sems.at[1, i]),
        )
        for copy in pair:
            copy.start()
        copies.append(pair)
    _, _, _, y = coordinates()
    for i in range(GROUPS):
        for copy in copies[i]:
            copy.wait()
        for j in range(GROUP_PAIRS):
            p = i * GROUP_PAIRS + j
            cols = pl.ds(p * LANES, LANES)
            state = pair_state(k_ref[:, cols], v_ref[:, cols])
            for c in range(QUARTERS):
                total_ref[y ^ c, p] = state[c * QROWS : (c + 1) * QROWS]


def totals(keys, values):
    return pl.pallas_call(
        totals_kernel,
        out_shape=(
            jax.ShapeDtypeStruct((QUARTERS, PAIRS, QROWS, LANES), jnp.float32),
            pltpu.VMEM((ROWS, HEADS * DK), jnp.bfloat16),
            pltpu.VMEM((ROWS, HEADS * DK), jnp.bfloat16),
        ),
        in_specs=[pl.BlockSpec(memory_space=pl.ANY)] * 2,
        out_specs=(pl.BlockSpec(memory_space=pltpu.VMEM),) * 3,
        scratch_shapes=[pltpu.SemaphoreType.DMA((2, GROUPS))],
        compiler_params=pltpu.CompilerParams(vmem_limit_bytes=12 << 20),
        name="totals",
    )(off_chip(keys), off_chip(values))


def inside_kernel(group, q_hbm, k_ref, v_ref, att_ref, before_ref, q_ref, run_ref, sem):
    start = group * GROUP_COLS
    copy = pltpu.make_async_copy(q_hbm.at[:, pl.ds(start, GROUP_COLS)], q_ref, sem)
    copy.start()
    run_ref[...] = jnp.zeros_like(run_ref)
    lane = lax.broadcasted_iota(jnp.int32, (BLOCK, LANES), 1)
    low = lane < DK
    row = lax.broadcasted_iota(jnp.int32, (BLOCK, 2 * BLOCK), 0)
    col = lax.broadcasted_iota(jnp.int32, (BLOCK, 2 * BLOCK), 1)
    causal = (col % BLOCK) <= row
    copy.wait()

    def block(b, _):
        rows = pl.ds(pl.multiple_of(b * BLOCK, BLOCK), BLOCK)
        for j in range(GROUP_PAIRS):
            here = pl.ds(j * LANES, LANES)
            cols = pl.ds(start + j * LANES, LANES)
            q, k, v = q_ref[rows, here], k_ref[rows, cols], v_ref[rows, cols]
            zero = jnp.zeros_like(k)
            k_both = jnp.concatenate([jnp.where(low, k, zero), jnp.where(low, zero, k)], 0)
            v_both = jnp.concatenate([jnp.where(low, v, zero), jnp.where(low, zero, v)], 0)
            scores = lax.dot_general(
                q, k_both, (((1,), (1,)), ((), ())), preferred_element_type=jnp.float32
            )
            weights = jnp.where(causal, scores, 0.0).astype(jnp.bfloat16)
            att_ref[rows, here] = jnp.dot(
                weights, v_both, preferred_element_type=jnp.float32
            )
            run = run_ref[j]
            before_ref[b, j] = run
            run_ref[j] = run + pair_state(k, v)
        return 0

    lax.fori_loop(0, BLOCKS, block, 0)


def inside(group, queries, keys, values):
    return pl.pallas_call(
        functools.partial(inside_kernel, group),
        out_shape=(
            pltpu.VMEM((ROWS, GROUP_COLS), jnp.float32),
            pltpu.VMEM((BLOCKS, GROUP_PAIRS, DK, LANES), jnp.float32),
            pltpu.VMEM((ROWS, GROUP_COLS), jnp.bfloat16),
        ),
        in_specs=[
            pl.BlockSpec(memory_space=pl.ANY),
            pl.BlockSpec(memory_space=pltpu.VMEM),
            pl.BlockSpec(memory_space=pltpu.VMEM),
        ],
        out_specs=(pl.BlockSpec(memory_space=pltpu.VMEM),) * 3,
        scratch_shapes=[
            pltpu.VMEM((GROUP_PAIRS, DK, LANES), jnp.float32),
            pltpu.SemaphoreType.DMA(()),
        ],
        compiler_params=pltpu.CompilerParams(vmem_limit_bytes=12 << 20),
        cost_estimate=pl.CostEstimate(
            flops=400_000_000, bytes_accessed=8 << 20, transcendentals=0
        ),
    )(off_chip(queries), on_chip(keys), on_chip(values))


def output_kernel(*refs):
    prefix_refs, refs = refs[:QUARTERS], refs[QUARTERS:]
    att_refs, refs = refs[:GROUPS], refs[GROUPS:]
    before_refs, refs = refs[:GROUPS], refs[GROUPS:]
    q_refs, refs = refs[:GROUPS], refs[GROUPS:]
    final_ref, gain_ref, mixed_hbm, final_out, prefix, stage, sems = refs
    _, _, x, y = coordinates()
    lane = lax.broadcasted_iota(jnp.int32, (8, LANES), 1)
    even, odd = final_ref[pl.ds(0, 8, stride=2)], final_ref[pl.ds(1, 8, stride=2)]
    first = jnp.where(lane < DK, even, pltpu.roll(odd, DK, 1))
    second = jnp.where(lane < DK, pltpu.roll(even, DK, 1), odd)
    final_out[...] = jnp.where(x % 2 == 0, first, second) * float(ROWS * 128) ** (-0.5)
    for c in range(QUARTERS):
        prefix[y ^ c] = prefix_refs[c][...]
    wide = 2 * LANES
    owner_row = lax.broadcasted_iota(jnp.int32, (wide, wide), 0) // DK
    owner_col = lax.broadcasted_iota(jnp.int32, (wide, wide), 1) // DK
    average = jnp.where(owner_row == owner_col, 1.0 / DK, 0.0).astype(jnp.bfloat16)
    lane = lax.broadcasted_iota(jnp.int32, (DK, LANES), 1)
    low = lane < DK
    nothing = jnp.zeros((LANES, LANES), jnp.bfloat16)

    def out_copy(b, slot):
        rows = pl.ds(pl.multiple_of(b * BLOCK, BLOCK), BLOCK)
        return pltpu.make_async_copy(stage.at[slot], mixed_hbm.at[rows], sems.at[slot])

    def block(b, _):
        slot = b % 2
        rows = pl.ds(pl.multiple_of(b * BLOCK, BLOCK), BLOCK)

        @pl.when(b >= 2)
        def _():
            out_copy(b - 2, slot).wait()

        for quad in range(PAIRS // 2):
            group, inner = divmod(quad * 2, GROUP_PAIRS)
            halves = []
            for j in range(2):
                p = quad * 2 + j
                before = jnp.concatenate([prefix[c, p] for c in range(QUARTERS)], 0)
                state = (before + before_refs[group][b, inner + j]).astype(jnp.bfloat16)
                zero = jnp.zeros_like(state)
                halves.append(
                    jnp.concatenate(
                        [jnp.where(low, state, zero), jnp.where(low, zero, state)], 0
                    )
                )
            states = jnp.concatenate(
                [
                    jnp.concatenate([halves[0], nothing], 1),
                    jnp.concatenate([nothing, halves[1]], 1),
                ],
                0,
            )
            here = pl.ds(inner * LANES, wide)
            cols = pl.ds(quad * wide, wide)
            attended = att_refs[group][rows, here] + jnp.dot(
                q_refs[group][rows, here], states, preferred_element_type=jnp.float32
            )
            mean = jnp.dot(
                (attended * attended).astype(jnp.bfloat16),
                average,
                preferred_element_type=jnp.float32,
            )
            scaled = attended * lax.rsqrt(mean + 1e-06) * gain_ref[:, cols]
            stage[slot, :, cols] = scaled.astype(jnp.bfloat16)
        out_copy(b, slot).start()
        return 0

    lax.fori_loop(0, BLOCKS, block, 0)
    for b in (BLOCKS - 2, BLOCKS - 1):
        out_copy(b, b % 2).wait()


def output(prefixes, atts, befores, qs, final, gain):
    in_vmem = pl.BlockSpec(memory_space=pltpu.VMEM)
    return pl.pallas_call(
        output_kernel,
        out_shape=(
            jax.ShapeDtypeStruct((ROWS, HEADS * DK), jnp.bfloat16),
            jax.ShapeDtypeStruct((8, LANES), jnp.float32),
        ),
        in_specs=[in_vmem] * (4 * GROUPS + 2),
        out_specs=(pl.BlockSpec(memory_space=pl.ANY), in_vmem),
        scratch_shapes=[
            pltpu.VMEM((QUARTERS, PAIRS, QROWS, LANES), jnp.float32),
            pltpu.VMEM((2, BLOCK, HEADS * DK), jnp.bfloat16),
            pltpu.SemaphoreType.DMA((2,)),
        ],
        compiler_params=pltpu.CompilerParams(vmem_limit_bytes=12 << 20),
        name="output",
    )(*prefixes, *map(on_chip, (*atts, *befores, *qs)), final, gain)


def keep(condition, array):
    return jnp.where(condition, array, jnp.zeros_like(array))


def plane_kernel(row_ref, core_ref, *refs):
    z, core, x, _ = coordinates()
    column, (before_ref, final_ref, *send_refs) = refs[:3], refs[3:]
    row_sum, other_core = row_ref[...], core_ref[...]
    before = keep(core == 1, other_core)
    for k in range(1, 4):
        before = before + keep((z ^ k) < z, column[k - 1][...])
    before_ref[...] = before

    def final_pair(k):
        p = (z * 2 + core) * 2 + (x ^ k) // 2
        chip = row_ref[p] + core_ref[p]
        return chip + (column[0][p] + column[1][p] + column[2][p])

    final_ref[...] = final_pair(0)
    for k in range(1, 4):
        send_refs[k - 1][:PAIRS] = before + keep(x < (x ^ k), row_sum)
        send_refs[k - 1][PAIRS] = final_pair(k)


def prefix_kernel(before_ref, final_ref, *refs):
    _, _, _, y = coordinates()
    plane, ring, sums, final_out = refs[:3], refs[3:7], refs[7:11], refs[11]
    rows_before = before_ref[...] + (
        plane[0][:PAIRS] + plane[1][:PAIRS] + plane[2][:PAIRS]
    )
    states = [r[...] for r in ring]
    for j in range(4):
        shorter = rows_before
        for k in range(4):
            if k != j:
                shorter = shorter + keep((y ^ k) < (y ^ j), states[k])
        sums[j][...] = shorter
    final_out[...] = final_ref[...] + (
        plane[0][PAIRS] + plane[1][PAIRS] + plane[2][PAIRS]
    )


def small_call(kernel, out_shapes, *args):
    in_vmem = pl.BlockSpec(memory_space=pltpu.VMEM)
    return pl.pallas_call(
        kernel,
        out_shape=[jax.ShapeDtypeStruct(s, jnp.float32) for s in out_shapes],
        in_specs=[in_vmem] * len(args),
        out_specs=[in_vmem] * len(out_shapes),
        compiler_params=pltpu.CompilerParams(vmem_limit_bytes=4 << 20),
    )(*args)


def steps(queries, key_rows, value_rows, norm_gain):
    total, keys, values = totals(key_rows, value_rows)
    pieces = []
    for g in range(GROUPS):
        pieces.append(inside(g, queries, keys, values))
    atts, befores, qs = zip(*pieces)

    ring = [total[0]] + [exchange(total[k], dy=k) for k in range(1, 4)]
    row_sum = (ring[0] + ring[1]) + (ring[2] + ring[3])
    other_core = exchange(row_sum, dc=1)
    chip_sum = row_sum + other_core
    column = [exchange(chip_sum, dz=k) for k in range(1, 4)]
    quarter = (PAIRS, QROWS, LANES)
    pair = (QROWS, LANES)
    before, final, *sends = small_call(
        plane_kernel,
        [quarter, pair] + [(PAIRS + 1, QROWS, LANES)] * 3,
        row_sum,
        other_core,
        *column,
    )
    plane = [exchange(sends[k - 1], dx=k) for k in range(1, 4)]
    *sums, final = small_call(prefix_kernel, [quarter] * 4 + [pair], before, final, *plane, *ring)
    prefixes = [sums[0]] + [exchange(sums[k], dy=k) for k in range(1, 4)]
    mixed, final_state = output(
        prefixes, atts, befores, qs, final, norm_gain.reshape(1, HEADS * DK)
    )
    return (mixed, final_state.reshape(8 * LANES))


def solution(mesh):
    return jax.shard_map(
        steps,
        mesh=mesh,
        in_specs=(P(AXES, None), P(AXES, None), P(AXES, None), P()),
        out_specs=(P(AXES, None), P(AXES)),
        check_vma=False,
    )
```

```python
import functools

import jax
import jax.numpy as jnp
from jax import lax
from jax.experimental import pallas as pl
from jax.experimental.pallas import tpu as pltpu
from jax.sharding import PartitionSpec as P


HEADS = 32
DK = 64
BLOCK = 128
LANES = 128
PAIRS = 16
ROWS = 1024
BLOCKS = ROWS // BLOCK
GROUPS = 4
GROUP_PAIRS = PAIRS // GROUPS
GROUP_COLS = GROUP_PAIRS * LANES
QUARTERS = 4
QROWS = DK // QUARTERS
WIDTH = HEADS * DK
AXES = ("outer", "inner")
IN_VMEM = pl.BlockSpec(memory_space=pltpu.VMEM)


def coordinates():
    outer, inner = lax.axis_index("outer"), lax.axis_index("inner")
    return outer // 2, outer % 2, inner // 4, inner % 4


def exchange(array, dz=0, dc=0, dx=0, dy=0):
    turn = ((dz * 2 + dc) * 4 + dx) * 4 + dy
    return lax.ppermute(array, AXES, [(rank, rank ^ turn) for rank in range(128)])


def on_chip(array):
    return pltpu.with_memory_space_constraint(array, pltpu.VMEM)


def off_chip(array):
    return pltpu.with_memory_space_constraint(array, pltpu.HBM)


def totals_kernel(k_hbm, v_hbm, total_ref, kt_ref, v_ref, k_ref, sems):
    copies = []
    for i in range(GROUPS):
        cols = pl.ds(i * GROUP_COLS, GROUP_COLS)
        pair = (
            pltpu.make_async_copy(k_hbm.at[:, cols], k_ref.at[:, cols], sems.at[0, i]),
            pltpu.make_async_copy(v_hbm.at[:, cols], v_ref.at[:, cols], sems.at[1, i]),
        )
        for copy in pair:
            copy.start()
        copies.append(pair)
    _, _, _, y = coordinates()
    low = lax.broadcasted_iota(jnp.int32, (DK, LANES), 1) < DK
    for i in range(GROUPS):
        for copy in copies[i]:
            copy.wait()
        for j in range(GROUP_PAIRS):
            p = i * GROUP_PAIRS + j
            cols = pl.ds(p * LANES, LANES)
            keys = k_ref[:, cols].T
            kt_ref[cols, :] = keys
            full = jnp.dot(keys, v_ref[:, cols], preferred_element_type=jnp.float32)
            state = jnp.where(low, full[:DK], full[DK:])
            for c in range(QUARTERS):
                total_ref[y ^ c, p] = state[c * QROWS : (c + 1) * QROWS]


def totals(keys, values):
    return pl.pallas_call(
        totals_kernel,
        out_shape=(
            jax.ShapeDtypeStruct((QUARTERS, PAIRS, QROWS, LANES), jnp.float32),
            pltpu.VMEM((WIDTH, ROWS), jnp.bfloat16),
            pltpu.VMEM((ROWS, WIDTH), jnp.bfloat16),
        ),
        in_specs=[pl.BlockSpec(memory_space=pl.ANY)] * 2,
        out_specs=(IN_VMEM,) * 3,
        scratch_shapes=[
            pltpu.VMEM((ROWS, WIDTH), jnp.bfloat16),
            pltpu.SemaphoreType.DMA((2, GROUPS)),
        ],
        compiler_params=pltpu.CompilerParams(vmem_limit_bytes=16 << 20),
        name="totals",
    )(off_chip(keys), off_chip(values))


def beside(state):
    low = lax.broadcasted_iota(jnp.int32, state.shape, 1) < DK
    zero = jnp.zeros_like(state)
    return jnp.concatenate([jnp.where(low, state, zero), jnp.where(low, zero, state)], 0)


def inside_kernel(group, *refs):
    q_hbm, refs = refs[0], refs[1:]
    q_ref = None
    if group > 0:
        q_ref, refs = refs[0], refs[1:]
    (kt_ref, v_ref, att_ref, before_ref), refs = refs[:4], refs[4:]
    start = group * GROUP_COLS
    *q_refs, mask_ref, sems = refs
    if group == 0:
        q_ref, q_refs = q_refs[0], q_refs[1:]
        own = pltpu.make_async_copy(q_hbm.at[:, pl.ds(0, GROUP_COLS)], q_ref, sems.at[0])
        own.start()
    if group < GROUPS - 1:
        ahead = pltpu.make_async_copy(
            q_hbm.at[:, pl.ds(start + GROUP_COLS, GROUP_COLS)], q_refs[0], sems.at[1]
        )
        ahead.start()
    row = lax.broadcasted_iota(jnp.int32, (BLOCK, 2 * BLOCK), 0)
    col = lax.broadcasted_iota(jnp.int32, (BLOCK, 2 * BLOCK), 1)
    mask_ref[...] = jnp.where((col % BLOCK) <= row, 1.0, 0.0).astype(jnp.bfloat16)
    half = jnp.zeros((DK, BLOCK), jnp.bfloat16)
    before = [jnp.zeros((DK, LANES), jnp.float32)] * GROUP_PAIRS
    if group == 0:
        own.wait()
    for b in range(BLOCKS):
        rows = pl.ds(b * BLOCK, BLOCK)
        last = b == BLOCKS - 1
        for j in range(GROUP_PAIRS):
            here = pl.ds(j * LANES, LANES)
            cols = pl.ds(start + j * LANES, LANES)
            q, keys, values = q_ref[rows, here], kt_ref[cols, rows], v_ref[rows, cols]
            first, second = keys[:DK], keys[DK:]
            k_both = jnp.concatenate(
                [
                    jnp.concatenate([first, half], 1),
                    jnp.concatenate([half, second], 1),
                ],
                0,
            )
            v_both = beside(values)
            scores = jnp.dot(q, k_both, preferred_element_type=jnp.float32)
            weights = scores.astype(jnp.bfloat16) * mask_ref[...]
            left = weights
            if not last:
                left = jnp.concatenate([weights, jnp.concatenate([first, second], 1)], 0)
            both = jnp.dot(left, v_both, preferred_element_type=jnp.float32)
            att_ref[rows, here] = both[:BLOCK]
            before_ref[b, j] = before[j]
            if not last:
                before[j] = before[j] + both[BLOCK:]
    if group < GROUPS - 1:
        ahead.wait()


def inside(group, queries, q_part, keys, values):
    part = pltpu.VMEM((ROWS, GROUP_COLS), jnp.bfloat16)
    fetched = (group == 0) + (group < GROUPS - 1)
    given = [] if q_part is None else [on_chip(q_part)]
    return pl.pallas_call(
        functools.partial(inside_kernel, group),
        out_shape=(
            pltpu.VMEM((ROWS, GROUP_COLS), jnp.float32),
            pltpu.VMEM((BLOCKS, GROUP_PAIRS, DK, LANES), jnp.float32),
        )
        + (part,) * fetched,
        in_specs=[pl.BlockSpec(memory_space=pl.ANY)] + [IN_VMEM] * (len(given) + 2),
        out_specs=(IN_VMEM,) * (2 + fetched),
        scratch_shapes=[
            pltpu.VMEM((BLOCK, 2 * BLOCK), jnp.bfloat16),
            pltpu.SemaphoreType.DMA((2,)),
        ],
        compiler_params=pltpu.CompilerParams(vmem_limit_bytes=10 << 20),
        cost_estimate=pl.CostEstimate(
            flops=400_000_000, bytes_accessed=8 << 20, transcendentals=0
        ),
    )(off_chip(queries), *given, on_chip(keys), on_chip(values))


def output_kernel(*refs):
    prefix_refs, refs = refs[:QUARTERS], refs[QUARTERS:]
    att_refs, refs = refs[:GROUPS], refs[GROUPS:]
    before_refs, refs = refs[:GROUPS], refs[GROUPS:]
    q_refs, refs = refs[:GROUPS], refs[GROUPS:]
    final_ref, gain_ref, mixed_hbm, final_out, prefix, stage, sems = refs
    _, _, x, y = coordinates()
    lane = lax.broadcasted_iota(jnp.int32, (8, LANES), 1)
    even, odd = final_ref[pl.ds(0, 8, stride=2)], final_ref[pl.ds(1, 8, stride=2)]
    first = jnp.where(lane < DK, even, pltpu.roll(odd, DK, 1))
    second = jnp.where(lane < DK, pltpu.roll(even, DK, 1), odd)
    final_out[...] = jnp.where(x % 2 == 0, first, second) * float(ROWS * 128) ** (-0.5)
    for c in range(QUARTERS):
        prefix[y ^ c] = prefix_refs[c][...]
    wide = 2 * LANES
    owner_row = lax.broadcasted_iota(jnp.int32, (wide, wide), 0) // DK
    owner_col = lax.broadcasted_iota(jnp.int32, (wide, wide), 1) // DK
    average = jnp.where(owner_row == owner_col, 1.0 / DK, 0.0).astype(jnp.bfloat16)
    nothing = jnp.zeros((LANES, LANES), jnp.bfloat16)
    copies = []
    for quad in range(PAIRS // 2):
        group, inner = divmod(quad * 2, GROUP_PAIRS)
        whole = [
            jnp.concatenate([prefix[c, quad * 2 + j] for c in range(QUARTERS)], 0)
            for j in range(2)
        ]
        here = pl.ds(inner * LANES, wide)
        cols = pl.ds(quad * wide, wide)
        parts = []
        for b in range(BLOCKS):
            rows = pl.ds(b * BLOCK, BLOCK)
            pair, other = (
                beside((whole[j] + before_refs[group][b, inner + j]).astype(jnp.bfloat16))
                for j in range(2)
            )
            states = jnp.concatenate(
                [
                    jnp.concatenate([pair, nothing], 1),
                    jnp.concatenate([nothing, other], 1),
                ],
                0,
            )
            carried = jnp.dot(
                q_refs[group][rows, here], states, preferred_element_type=jnp.float32
            )
            parts.append(att_refs[group][rows, here] + carried)
        attended = jnp.concatenate(parts, 0)
        mean = jnp.dot(
            (attended * attended).astype(jnp.bfloat16),
            average,
            preferred_element_type=jnp.float32,
        )
        scale = lax.rsqrt(mean + 1e-06) * gain_ref[:, cols]
        stage[:, cols] = (attended * scale).astype(jnp.bfloat16)
        copy = pltpu.make_async_copy(stage.at[:, cols], mixed_hbm.at[:, cols], sems.at[quad])
        copy.start()
        copies.append(copy)
    for copy in copies:
        copy.wait()


def output(prefixes, atts, befores, qs, final, gain):
    return pl.pallas_call(
        output_kernel,
        out_shape=(
            jax.ShapeDtypeStruct((ROWS, WIDTH), jnp.bfloat16),
            jax.ShapeDtypeStruct((8, LANES), jnp.float32),
        ),
        in_specs=[IN_VMEM] * (QUARTERS + 3 * GROUPS + 2),
        out_specs=(pl.BlockSpec(memory_space=pl.ANY), IN_VMEM),
        scratch_shapes=[
            pltpu.VMEM((QUARTERS, PAIRS, QROWS, LANES), jnp.float32),
            pltpu.VMEM((ROWS, WIDTH), jnp.bfloat16),
            pltpu.SemaphoreType.DMA((PAIRS // 2,)),
        ],
        compiler_params=pltpu.CompilerParams(vmem_limit_bytes=12 << 20),
        name="output",
    )(*prefixes, *map(on_chip, (*atts, *befores, *qs)), final, gain)


def keep(condition, array):
    return jnp.where(condition, array, jnp.zeros_like(array))


def plane_kernel(row_ref, core_ref, *refs):
    z, core, x, _ = coordinates()
    column, (before_ref, final_ref, *send_refs) = refs[:3], refs[3:]
    row_sum, other_core = row_ref[...], core_ref[...]
    before = keep(core == 1, other_core)
    for k in range(1, 4):
        before = before + keep((z ^ k) < z, column[k - 1][...])
    before_ref[...] = before

    def final_pair(k):
        p = (z * 2 + core) * 2 + (x ^ k) // 2
        chip = row_ref[p] + core_ref[p]
        return chip + (column[0][p] + column[1][p] + column[2][p])

    final_ref[...] = final_pair(0)
    for k in range(1, 4):
        send_refs[k - 1][:PAIRS] = before + keep(x < (x ^ k), row_sum)
        send_refs[k - 1][PAIRS] = final_pair(k)


def prefix_kernel(before_ref, final_ref, *refs):
    _, _, _, y = coordinates()
    plane, ring, sums, final_out = refs[:3], refs[3:7], refs[7:11], refs[11]
    rows_before = before_ref[...] + (
        plane[0][:PAIRS] + plane[1][:PAIRS] + plane[2][:PAIRS]
    )
    states = [r[...] for r in ring]
    for j in range(4):
        shorter = rows_before
        for k in range(4):
            if k != j:
                shorter = shorter + keep((y ^ k) < (y ^ j), states[k])
        sums[j][...] = shorter
    final_out[...] = final_ref[...] + (
        plane[0][PAIRS] + plane[1][PAIRS] + plane[2][PAIRS]
    )


def small_call(kernel, out_shapes, *args):
    return pl.pallas_call(
        kernel,
        out_shape=[jax.ShapeDtypeStruct(s, jnp.float32) for s in out_shapes],
        in_specs=[IN_VMEM] * len(args),
        out_specs=[IN_VMEM] * len(out_shapes),
        compiler_params=pltpu.CompilerParams(vmem_limit_bytes=4 << 20),
    )(*args)


def steps(queries, key_rows, value_rows, norm_gain):
    total, keys, values = totals(key_rows, value_rows)
    atts, befores, qs = [], [], []
    for g in range(GROUPS):
        attended, before, *fetched = inside(g, queries, qs[g] if g else None, keys, values)
        atts.append(attended)
        befores.append(before)
        qs.extend(fetched)

    ring = [total[0]] + [exchange(total[k], dy=k) for k in range(1, 4)]
    row_sum = (ring[0] + ring[1]) + (ring[2] + ring[3])
    other_core = exchange(row_sum, dc=1)
    chip_sum = row_sum + other_core
    column = [exchange(chip_sum, dz=k) for k in range(1, 4)]
    quarter = (PAIRS, QROWS, LANES)
    pair = (QROWS, LANES)
    before, final, *sends = small_call(
        plane_kernel,
        [quarter, pair] + [(PAIRS + 1, QROWS, LANES)] * 3,
        row_sum,
        other_core,
        *column,
    )
    plane = [exchange(sends[k - 1], dx=k) for k in range(1, 4)]
    *sums, final = small_call(prefix_kernel, [quarter] * 4 + [pair], before, final, *plane, *ring)
    prefixes = [sums[0]] + [exchange(sums[k], dy=k) for k in range(1, 4)]
    mixed, final_state = output(
        prefixes, atts, befores, qs, final, norm_gain.reshape(1, WIDTH)
    )
    return (mixed, final_state.reshape(8 * LANES))


def solution(mesh):
    return jax.shard_map(
        steps,
        mesh=mesh,
        in_specs=(P(AXES, None), P(AXES, None), P(AXES, None), P()),
        out_specs=(P(AXES, None), P(AXES)),
        check_vma=False,
    )
```

```python
import functools

import jax
import jax.numpy as jnp
from jax import lax
from jax.experimental import pallas as pl
from jax.experimental.pallas import tpu as pltpu
from jax.sharding import PartitionSpec as P


HEADS = 32
DK = 64
BLOCK = 128
LANES = 128
PAIRS = 16
ROWS = 1024
BLOCKS = ROWS // BLOCK
GROUPS = 4
GROUP_PAIRS = PAIRS // GROUPS
GROUP_COLS = GROUP_PAIRS * LANES
QUARTERS = 4
QROWS = DK // QUARTERS
WIDTH = HEADS * DK
AXES = ("outer", "inner")
IN_VMEM = pl.BlockSpec(memory_space=pltpu.VMEM)


def coordinates():
    outer, inner = lax.axis_index("outer"), lax.axis_index("inner")
    return outer // 2, outer % 2, inner // 4, inner % 4


def exchange(array, dz=0, dc=0, dx=0, dy=0):
    turn = ((dz * 2 + dc) * 4 + dx) * 4 + dy
    return lax.ppermute(array, AXES, [(rank, rank ^ turn) for rank in range(128)])


def on_chip(array):
    return pltpu.with_memory_space_constraint(array, pltpu.VMEM)


def off_chip(array):
    return pltpu.with_memory_space_constraint(array, pltpu.HBM)


def totals_kernel(k_hbm, v_hbm, total_ref, kt_ref, v_ref, k_ref, sems):
    copies = []
    for i in range(GROUPS):
        cols = pl.ds(i * GROUP_COLS, GROUP_COLS)
        pair = (
            pltpu.make_async_copy(k_hbm.at[:, cols], k_ref.at[:, cols], sems.at[0, i]),
            pltpu.make_async_copy(v_hbm.at[:, cols], v_ref.at[:, cols], sems.at[1, i]),
        )
        for copy in pair:
            copy.start()
        copies.append(pair)
    _, _, _, y = coordinates()
    low = lax.broadcasted_iota(jnp.int32, (DK, LANES), 1) < DK
    for i in range(GROUPS):
        for copy in copies[i]:
            copy.wait()
        for j in range(GROUP_PAIRS):
            p = i * GROUP_PAIRS + j
            cols = pl.ds(p * LANES, LANES)
            keys = k_ref[:, cols].T
            kt_ref[cols, :] = keys
            full = jnp.dot(keys, v_ref[:, cols], preferred_element_type=jnp.float32)
            state = jnp.where(low, full[:DK], full[DK:])
            for c in range(QUARTERS):
                total_ref[y ^ c, p] = state[c * QROWS : (c + 1) * QROWS]


def totals(keys, values):
    return pl.pallas_call(
        totals_kernel,
        out_shape=(
            jax.ShapeDtypeStruct((QUARTERS, PAIRS, QROWS, LANES), jnp.float32),
            pltpu.VMEM((WIDTH, ROWS), jnp.bfloat16),
            pltpu.VMEM((ROWS, WIDTH), jnp.bfloat16),
        ),
        in_specs=[pl.BlockSpec(memory_space=pl.ANY)] * 2,
        out_specs=(IN_VMEM,) * 3,
        scratch_shapes=[
            pltpu.VMEM((ROWS, WIDTH), jnp.bfloat16),
            pltpu.SemaphoreType.DMA((2, GROUPS)),
        ],
        compiler_params=pltpu.CompilerParams(vmem_limit_bytes=16 << 20),
        name="totals",
    )(off_chip(keys), off_chip(values))


def beside(state):
    low = lax.broadcasted_iota(jnp.int32, state.shape, 1) < DK
    zero = jnp.zeros_like(state)
    return jnp.concatenate([jnp.where(low, state, zero), jnp.where(low, zero, state)], 0)


def inside_kernel(group, *refs):
    q_hbm, refs = refs[0], refs[1:]
    q_ref = None
    if group > 0:
        q_ref, refs = refs[0], refs[1:]
    (kt_ref, v_ref, att_ref, before_ref), refs = refs[:4], refs[4:]
    start = group * GROUP_COLS
    *q_refs, mask_ref, sems = refs
    if group == 0:
        q_ref, q_refs = q_refs[0], q_refs[1:]
        own = pltpu.make_async_copy(q_hbm.at[:, pl.ds(0, GROUP_COLS)], q_ref, sems.at[0])
        own.start()
    if group < GROUPS - 1:
        ahead = pltpu.make_async_copy(
            q_hbm.at[:, pl.ds(start + GROUP_COLS, GROUP_COLS)], q_refs[0], sems.at[1]
        )
        ahead.start()
    row = lax.broadcasted_iota(jnp.int32, (BLOCK, 2 * BLOCK), 0)
    col = lax.broadcasted_iota(jnp.int32, (BLOCK, 2 * BLOCK), 1)
    mask_ref[...] = jnp.where((col % BLOCK) <= row, 1.0, 0.0).astype(jnp.bfloat16)
    half = jnp.zeros((DK, BLOCK), jnp.bfloat16)
    before = [jnp.zeros((DK, LANES), jnp.float32)] * GROUP_PAIRS
    if group == 0:
        own.wait()
    for b in range(BLOCKS):
        rows = pl.ds(b * BLOCK, BLOCK)
        last = b == BLOCKS - 1
        for j in range(GROUP_PAIRS):
            here = pl.ds(j * LANES, LANES)
            cols = pl.ds(start + j * LANES, LANES)
            q, keys, values = q_ref[rows, here], kt_ref[cols, rows], v_ref[rows, cols]
            first, second = keys[:DK], keys[DK:]
            k_both = jnp.concatenate(
                [
                    jnp.concatenate([first, half], 1),
                    jnp.concatenate([half, second], 1),
                ],
                0,
            )
            v_both = beside(values)
            scores = jnp.dot(q, k_both, preferred_element_type=jnp.float32)
            weights = scores.astype(jnp.bfloat16) * mask_ref[...]
            left = weights
            if not last:
                left = jnp.concatenate([weights, jnp.concatenate([first, second], 1)], 0)
            both = jnp.dot(left, v_both, preferred_element_type=jnp.float32)
            att_ref[rows, here] = both[:BLOCK]
            before_ref[b, j] = before[j]
            if not last:
                before[j] = before[j] + both[BLOCK:]
    if group < GROUPS - 1:
        ahead.wait()


def inside(group, queries, q_part, keys, values):
    part = pltpu.VMEM((ROWS, GROUP_COLS), jnp.bfloat16)
    fetched = (group == 0) + (group < GROUPS - 1)
    given = [] if q_part is None else [on_chip(q_part)]
    return pl.pallas_call(
        functools.partial(inside_kernel, group),
        out_shape=(
            pltpu.VMEM((ROWS, GROUP_COLS), jnp.float32),
            pltpu.VMEM((BLOCKS, GROUP_PAIRS, DK, LANES), jnp.float32),
        )
        + (part,) * fetched,
        in_specs=[pl.BlockSpec(memory_space=pl.ANY)] + [IN_VMEM] * (len(given) + 2),
        out_specs=(IN_VMEM,) * (2 + fetched),
        scratch_shapes=[
            pltpu.VMEM((BLOCK, 2 * BLOCK), jnp.bfloat16),
            pltpu.SemaphoreType.DMA((2,)),
        ],
        compiler_params=pltpu.CompilerParams(vmem_limit_bytes=10 << 20),
        cost_estimate=pl.CostEstimate(
            flops=400_000_000, bytes_accessed=8 << 20, transcendentals=0
        ),
    )(off_chip(queries), *given, on_chip(keys), on_chip(values))


def output_kernel(*refs):
    prefix_refs, refs = refs[:QUARTERS], refs[QUARTERS:]
    att_refs, refs = refs[:GROUPS], refs[GROUPS:]
    before_refs, refs = refs[:GROUPS], refs[GROUPS:]
    q_refs, refs = refs[:GROUPS], refs[GROUPS:]
    final_ref, gain_ref, mixed_hbm, final_out, prefix, stage, sems = refs
    _, _, x, y = coordinates()
    lane = lax.broadcasted_iota(jnp.int32, (8, LANES), 1)
    even, odd = final_ref[pl.ds(0, 8, stride=2)], final_ref[pl.ds(1, 8, stride=2)]
    first = jnp.where(lane < DK, even, pltpu.roll(odd, DK, 1))
    second = jnp.where(lane < DK, pltpu.roll(even, DK, 1), odd)
    final_out[...] = jnp.where(x % 2 == 0, first, second) * float(ROWS * 128) ** (-0.5)
    for c in range(QUARTERS):
        prefix[y ^ c] = prefix_refs[c][...]
    wide = 2 * LANES
    owner_row = lax.broadcasted_iota(jnp.int32, (wide, wide), 0) // DK
    owner_col = lax.broadcasted_iota(jnp.int32, (wide, wide), 1) // DK
    average = jnp.where(owner_row == owner_col, 1.0 / DK, 0.0).astype(jnp.bfloat16)
    nothing = jnp.zeros((LANES, LANES), jnp.bfloat16)
    copies = []
    for quad in range(PAIRS // 2):
        group, inner = divmod(quad * 2, GROUP_PAIRS)
        whole = [
            jnp.concatenate([prefix[c, quad * 2 + j] for c in range(QUARTERS)], 0)
            for j in range(2)
        ]
        here = pl.ds(inner * LANES, wide)
        cols = pl.ds(quad * wide, wide)
        parts = []
        for b in range(BLOCKS):
            rows = pl.ds(b * BLOCK, BLOCK)
            pair, other = (
                beside((whole[j] + before_refs[group][b, inner + j]).astype(jnp.bfloat16))
                for j in range(2)
            )
            states = jnp.concatenate(
                [
                    jnp.concatenate([pair, nothing], 1),
                    jnp.concatenate([nothing, other], 1),
                ],
                0,
            )
            carried = jnp.dot(
                q_refs[group][rows, here], states, preferred_element_type=jnp.float32
            )
            parts.append(att_refs[group][rows, here] + carried)
        attended = jnp.concatenate(parts, 0)
        mean = jnp.dot(
            (attended * attended).astype(jnp.bfloat16),
            average,
            preferred_element_type=jnp.float32,
        )
        scale = lax.rsqrt(mean + 1e-06) * gain_ref[:, cols]
        stage[:, cols] = (attended * scale).astype(jnp.bfloat16)
        copy = pltpu.make_async_copy(stage.at[:, cols], mixed_hbm.at[:, cols], sems.at[quad])
        copy.start()
        copies.append(copy)
    for copy in copies:
        copy.wait()


def output(prefixes, atts, befores, qs, final, gain):
    return pl.pallas_call(
        output_kernel,
        out_shape=(
            jax.ShapeDtypeStruct((ROWS, WIDTH), jnp.bfloat16),
            jax.ShapeDtypeStruct((8, LANES), jnp.float32),
        ),
        in_specs=[IN_VMEM] * (QUARTERS + 3 * GROUPS + 2),
        out_specs=(pl.BlockSpec(memory_space=pl.ANY), IN_VMEM),
        scratch_shapes=[
            pltpu.VMEM((QUARTERS, PAIRS, QROWS, LANES), jnp.float32),
            pltpu.VMEM((ROWS, WIDTH), jnp.bfloat16),
            pltpu.SemaphoreType.DMA((PAIRS // 2,)),
        ],
        compiler_params=pltpu.CompilerParams(vmem_limit_bytes=12 << 20),
        name="output",
    )(*prefixes, *map(on_chip, (*atts, *befores, *qs)), final, gain)


def keep(condition, array):
    return jnp.where(condition, array, jnp.zeros_like(array))


def line_kernel(row_ref, *refs):
    _, core, x, _ = coordinates()
    line, (before_ref, mine_ref, other_ref) = refs[:3], refs[3:]
    before = jnp.zeros(row_ref.shape, jnp.float32)
    for k in range(1, 4):
        before = before + keep((x ^ k) < x, line[k - 1][...])
    before_ref[...] = before
    plane = (row_ref[...] + line[0][...]) + (line[1][...] + line[2][...])
    for i in range(PAIRS // 4):
        zero, one = plane[i * 4 : i * 4 + 2], plane[i * 4 + 2 : i * 4 + 4]
        mine_ref[i * 2 : i * 2 + 2] = jnp.where(core == 0, zero, one)
        other_ref[i * 2 : i * 2 + 2] = jnp.where(core == 0, one, zero)


def column_kernel(mine_ref, got_ref, *refs):
    z, core, x, _ = coordinates()
    column, (own_ref, send_ref, final_ref) = refs[:3], refs[3:]
    mine, got = mine_ref[...], got_ref[...]
    below = jnp.zeros_like(mine)
    for k in range(1, 4):
        below = below + keep((z ^ k) < z, column[k - 1][...])
    own_ref[...] = below + keep(core == 1, got)
    send_ref[...] = below + keep(core == 0, mine)
    p = z * 2 + x // 2
    chip = mine_ref[p] + got_ref[p]
    final_ref[...] = chip + (column[0][p] + column[1][p] + column[2][p])


def prefix_kernel(before_ref, own_ref, other_ref, *refs):
    _, core, _, y = coordinates()
    ring, sums, rows_before = refs[:4], refs[4:8], refs[8]
    for i in range(PAIRS // 4):
        for half, ref in ((core, own_ref), (1 - core, other_ref)):
            pairs = pl.ds(i * 4 + half * 2, 2)
            rows_before[pairs] = before_ref[pairs] + ref[i * 2 : i * 2 + 2]
    states = [r[...] for r in ring]
    for j in range(4):
        shorter = rows_before[...]
        for k in range(4):
            if k != j:
                shorter = shorter + keep((y ^ k) < (y ^ j), states[k])
        sums[j][...] = shorter


def small_call(kernel, out_shapes, *args, scratch=()):
    return pl.pallas_call(
        kernel,
        out_shape=[jax.ShapeDtypeStruct(s, jnp.float32) for s in out_shapes],
        in_specs=[IN_VMEM] * len(args),
        out_specs=[IN_VMEM] * len(out_shapes),
        scratch_shapes=scratch,
        compiler_params=pltpu.CompilerParams(vmem_limit_bytes=4 << 20),
    )(*args)


def steps(queries, key_rows, value_rows, norm_gain):
    total, keys, values = totals(key_rows, value_rows)
    atts, befores, qs = [], [], []
    for g in range(GROUPS):
        attended, before, *fetched = inside(g, queries, qs[g] if g else None, keys, values)
        atts.append(attended)
        befores.append(before)
        qs.extend(fetched)

    ring = [total[0]] + [exchange(total[k], dy=k) for k in range(1, 4)]
    row_sum = (ring[0] + ring[1]) + (ring[2] + ring[3])
    line = [exchange(row_sum, dx=k) for k in range(1, 4)]
    quarter, half = (PAIRS, QROWS, LANES), (PAIRS // 2, QROWS, LANES)
    before, mine, other = small_call(line_kernel, [quarter, half, half], row_sum, *line)
    got = exchange(other, dc=1)
    chip_sum = mine + got
    column = [exchange(chip_sum, dz=k) for k in range(1, 4)]
    own, send, final = small_call(column_kernel, [half, half, (QROWS, LANES)], mine, got, *column)
    others = exchange(send, dc=1)
    sums = small_call(
        prefix_kernel,
        [quarter] * 4,
        before,
        own,
        others,
        *ring,
        scratch=[pltpu.VMEM(quarter, jnp.float32)],
    )
    prefixes = [sums[0]] + [exchange(sums[k], dy=k) for k in range(1, 4)]
    mixed, final_state = output(
        prefixes, atts, befores, qs, final, norm_gain.reshape(1, WIDTH)
    )
    return (mixed, final_state.reshape(8 * LANES))


def solution(mesh):
    return jax.shard_map(
        steps,
        mesh=mesh,
        in_specs=(P(AXES, None), P(AXES, None), P(AXES, None), P()),
        out_specs=(P(AXES, None), P(AXES)),
        check_vma=False,
    )
```

```python
import functools

import jax
import jax.numpy as jnp
from jax import lax
from jax.experimental import pallas as pl
from jax.experimental.pallas import tpu as pltpu
from jax.sharding import PartitionSpec as P


HEADS = 32
DK = 64
BLOCK = 128
LANES = 128
PAIRS = 16
ROWS = 1024
BLOCKS = ROWS // BLOCK
GROUPS = 4
GROUP_PAIRS = PAIRS // GROUPS
GROUP_COLS = GROUP_PAIRS * LANES
STATE_ROWS = GROUP_PAIRS * DK
TURNS = (0, 2, 3, 1)
SHARE_ROWS = DK // 4
WIDTH = HEADS * DK
AXES = ("outer", "inner")
IN_VMEM = pl.BlockSpec(memory_space=pltpu.VMEM)


def coordinates():
    outer, inner = lax.axis_index("outer"), lax.axis_index("inner")
    return outer // 2, outer % 2, inner // 4, inner % 4


def exchange(array, dz=0, dc=0, dx=0, dy=0):
    turn = ((dz * 2 + dc) * 4 + dx) * 4 + dy
    return lax.ppermute(array, AXES, [(rank, rank ^ turn) for rank in range(128)])


def on_chip(array):
    return pltpu.with_memory_space_constraint(array, pltpu.VMEM)


def off_chip(array):
    return pltpu.with_memory_space_constraint(array, pltpu.HBM)


def totals_kernel(k_hbm, v_hbm, total_ref, kt_ref, v_ref, k_ref, sems):
    copies = []
    for i in range(GROUPS):
        cols = pl.ds(i * GROUP_COLS, GROUP_COLS)
        pair = (
            pltpu.make_async_copy(k_hbm.at[:, cols], k_ref.at[:, cols], sems.at[0, i]),
            pltpu.make_async_copy(v_hbm.at[:, cols], v_ref.at[:, cols], sems.at[1, i]),
        )
        for copy in pair:
            copy.start()
        copies.append(pair)
    _, _, _, y = coordinates()
    low = lax.broadcasted_iota(jnp.int32, (DK, LANES), 1) < DK
    for i in range(GROUPS):
        for copy in copies[i]:
            copy.wait()
        for j in range(GROUP_PAIRS):
            p = i * GROUP_PAIRS + j
            cols = pl.ds(p * LANES, LANES)
            keys = k_ref[:, cols].T
            kt_ref[cols, :] = keys
            full = jnp.dot(keys, v_ref[:, cols], preferred_element_type=jnp.float32)
            state = jnp.where(low, full[:DK], full[DK:])
            total_ref[y ^ i, j * DK : (j + 1) * DK] = state


def totals(keys, values):
    return pl.pallas_call(
        totals_kernel,
        out_shape=(
            jax.ShapeDtypeStruct((GROUPS, STATE_ROWS, LANES), jnp.float32),
            pltpu.VMEM((WIDTH, ROWS), jnp.bfloat16),
            pltpu.VMEM((ROWS, WIDTH), jnp.bfloat16),
        ),
        in_specs=[pl.BlockSpec(memory_space=pl.ANY)] * 2,
        out_specs=(IN_VMEM,) * 3,
        scratch_shapes=[
            pltpu.VMEM((ROWS, WIDTH), jnp.bfloat16),
            pltpu.SemaphoreType.DMA((2, GROUPS)),
        ],
        compiler_params=pltpu.CompilerParams(vmem_limit_bytes=16 << 20),
        name="totals",
    )(off_chip(keys), off_chip(values))


def beside(state):
    low = lax.broadcasted_iota(jnp.int32, state.shape, 1) < DK
    zero = jnp.zeros_like(state)
    return jnp.concatenate([jnp.where(low, state, zero), jnp.where(low, zero, state)], 0)


def inside_kernel(group, *refs):
    _, _, _, y = coordinates()
    start = pl.multiple_of((y ^ TURNS[group]) * GROUP_COLS, GROUP_COLS)
    if group == 0:
        q_hbm, kt_ref, v_ref, att_ref, before_ref, q_ref, mask_ref, sems = refs
        fetches = []
        for k in range(GROUPS):
            cols = pl.ds(pl.multiple_of((y ^ TURNS[k]) * GROUP_COLS, GROUP_COLS), GROUP_COLS)
            fetches.append(
                pltpu.make_async_copy(q_hbm.at[:, cols], q_ref.at[:, cols], sems.at[k])
            )
            fetches[k].start()
    else:
        q_ref, kt_ref, v_ref, att_ref, before_ref, mask_ref = refs
    row = lax.broadcasted_iota(jnp.int32, (BLOCK, 2 * BLOCK), 0)
    col = lax.broadcasted_iota(jnp.int32, (BLOCK, 2 * BLOCK), 1)
    mask_ref[...] = jnp.where((col % BLOCK) <= row, 1.0, 0.0).astype(jnp.bfloat16)
    half = jnp.zeros((DK, BLOCK), jnp.bfloat16)
    before = [jnp.zeros((DK, LANES), jnp.float32)] * GROUP_PAIRS
    if group == 0:
        fetches[0].wait()
    for b in range(BLOCKS):
        rows = pl.ds(b * BLOCK, BLOCK)
        last = b == BLOCKS - 1
        for j in range(GROUP_PAIRS):
            here = pl.ds(j * LANES, LANES)
            cols = pl.ds(pl.multiple_of(start + j * LANES, LANES), LANES)
            q, keys, values = q_ref[rows, cols], kt_ref[cols, rows], v_ref[rows, cols]
            first, second = keys[:DK], keys[DK:]
            k_both = jnp.concatenate(
                [
                    jnp.concatenate([first, half], 1),
                    jnp.concatenate([half, second], 1),
                ],
                0,
            )
            v_both = beside(values)
            scores = jnp.dot(q, k_both, preferred_element_type=jnp.float32)
            weights = scores.astype(jnp.bfloat16) * mask_ref[...]
            left = weights
            if not last:
                left = jnp.concatenate([weights, jnp.concatenate([first, second], 1)], 0)
            both = jnp.dot(left, v_both, preferred_element_type=jnp.float32)
            att_ref[rows, here] = both[:BLOCK]
            before_ref[b, j] = before[j]
            if not last:
                before[j] = before[j] + both[BLOCK:]
    if group == 0:
        for fetch in fetches[1:]:
            fetch.wait()


def inside(group, queries, keys, values):
    out_shape = [
        pltpu.VMEM((ROWS, GROUP_COLS), jnp.float32),
        pltpu.VMEM((BLOCKS, GROUP_PAIRS, DK, LANES), jnp.float32),
    ]
    scratch = [pltpu.VMEM((BLOCK, 2 * BLOCK), jnp.bfloat16)]
    first = group == 0
    if first:
        out_shape.append(pltpu.VMEM((ROWS, WIDTH), jnp.bfloat16))
        scratch.append(pltpu.SemaphoreType.DMA((GROUPS,)))
    return pl.pallas_call(
        functools.partial(inside_kernel, group),
        out_shape=out_shape,
        in_specs=[pl.BlockSpec(memory_space=pl.ANY) if first else IN_VMEM] + [IN_VMEM] * 2,
        out_specs=[IN_VMEM] * len(out_shape),
        scratch_shapes=scratch,
        compiler_params=pltpu.CompilerParams(vmem_limit_bytes=10 << 20),
        cost_estimate=pl.CostEstimate(
            flops=400_000_000, bytes_accessed=8 << 20, transcendentals=0
        ),
    )((off_chip if first else on_chip)(queries), on_chip(keys), on_chip(values))


def normed(start, att_ref, before_ref, q_ref, gain_ref, prefix_ref, stage_ref, ready):
    wide = 2 * LANES
    owner_row = lax.broadcasted_iota(jnp.int32, (wide, wide), 0) // DK
    owner_col = lax.broadcasted_iota(jnp.int32, (wide, wide), 1) // DK
    average = jnp.where(owner_row == owner_col, 1.0 / DK, 0.0).astype(jnp.bfloat16)
    nothing = jnp.zeros((LANES, LANES), jnp.bfloat16)
    for quad in range(GROUP_PAIRS // 2):
        whole = [prefix_ref[pl.ds((quad * 2 + j) * DK, DK)] for j in range(2)]
        here = pl.ds(quad * wide, wide)
        cols = pl.ds(pl.multiple_of(start + quad * wide, wide), wide)
        parts = []
        for b in range(BLOCKS):
            rows = pl.ds(b * BLOCK, BLOCK)
            pair, other = (
                beside((whole[j] + before_ref[b, quad * 2 + j]).astype(jnp.bfloat16))
                for j in range(2)
            )
            states = jnp.concatenate(
                [
                    jnp.concatenate([pair, nothing], 1),
                    jnp.concatenate([nothing, other], 1),
                ],
                0,
            )
            carried = jnp.dot(q_ref[rows, cols], states, preferred_element_type=jnp.float32)
            parts.append(att_ref[rows, here] + carried)
        attended = jnp.concatenate(parts, 0)
        mean = jnp.dot(
            (attended * attended).astype(jnp.bfloat16),
            average,
            preferred_element_type=jnp.float32,
        )
        scale = lax.rsqrt(mean + 1e-06) * gain_ref[:, cols]
        stage_ref[:, here] = (attended * scale).astype(jnp.bfloat16)
        ready(quad)


def columns(group):
    _, _, _, y = coordinates()
    return pl.multiple_of((y ^ TURNS[group]) * GROUP_COLS, GROUP_COLS)


def plain_output(group, att, before, q, gain, prefix, stage):
    normed(columns(group), att, before, q, gain, prefix, stage, lambda quad: None)


def copying_output(group, att, before, q, gain, prefix, last_stage, mixed, stage, sem):
    copy = pltpu.make_async_copy(
        last_stage, mixed.at[:, pl.ds(columns(group - 1), GROUP_COLS)], sem
    )
    copy.start()
    plain_output(group, att, before, q, gain, prefix, stage)
    copy.wait()


def last_output(att, before, q, gain, prefix, *refs):
    stages, (first, second, third, _), refs = refs[:2], refs[2:6], refs[6:]
    mixed, final_out, stage, share, sems = refs
    group = GROUPS - 1
    start = columns(group)
    copies = []
    for k in (1, 2):
        cols = pl.ds(columns(k), GROUP_COLS)
        copies.append(pltpu.make_async_copy(stages[k - 1], mixed.at[:, cols], sems.at[k - 1]))
        copies[-1].start()

    def ready(quad):
        wide = 2 * LANES
        cols = pl.ds(pl.multiple_of(start + quad * wide, wide), wide)
        copy = pltpu.make_async_copy(
            stage.at[:, pl.ds(quad * wide, wide)], mixed.at[:, cols], sems.at[2 + quad]
        )
        copy.start()
        copies.append(copy)

    z, _, x, y = coordinates()
    tail = pl.ds(STATE_ROWS, SHARE_ROWS)
    rows = jnp.zeros((SHARE_ROWS, LANES), jnp.float32)
    for k, ref in zip(TURNS, (first, second, third, prefix)):
        rows = jnp.where((y ^ k) == z, ref[tail], rows)
    share[...] = jnp.where(x % 2 == 0, rows, pltpu.roll(rows, DK, 1))
    lane = lax.broadcasted_iota(jnp.int32, (8, LANES), 1)
    even, odd = share[pl.ds(0, 8, stride=2)], share[pl.ds(1, 8, stride=2)]
    final = jnp.where(lane < DK, even, pltpu.roll(odd, DK, 1))
    final_out[...] = final * float(ROWS * 128) ** (-0.5)

    normed(start, att, before, q, gain, prefix, stage, ready)
    for copy in copies:
        copy.wait()


def output(group, att, before, q, gain, prefixes, stages, mixed):
    part = pltpu.VMEM((ROWS, GROUP_COLS), jnp.bfloat16)
    whole = pltpu.HBM((ROWS, WIDTH), jnp.bfloat16)
    in_hbm = pl.BlockSpec(memory_space=pl.ANY)
    args = [*map(on_chip, (att, before, q)), gain, prefixes[group]]
    in_specs = [IN_VMEM] * len(args)
    kernel = functools.partial(plain_output, group)
    out_shape, out_specs, scratch, aliases = [part], [IN_VMEM], [], {}
    if group == 1:
        kernel = functools.partial(copying_output, group)
        args.append(on_chip(stages[0]))
        in_specs.append(IN_VMEM)
        out_shape, out_specs = [whole, part], [in_hbm, IN_VMEM]
        scratch = [pltpu.SemaphoreType.DMA(())]
    elif group == GROUPS - 1:
        kernel = last_output
        args.extend([on_chip(stages[1]), on_chip(stages[2]), *prefixes[:group]])
        in_specs.extend([IN_VMEM] * (2 + group) + [in_hbm])
        aliases = {len(args): 0}
        args.append(off_chip(mixed))
        out_shape = [whole, jax.ShapeDtypeStruct((8, LANES), jnp.float32)]
        out_specs = [in_hbm, IN_VMEM]
        scratch = [
            part,
            pltpu.VMEM((SHARE_ROWS, LANES), jnp.float32),
            pltpu.SemaphoreType.DMA((2 + GROUP_PAIRS // 2,)),
        ]
    return pl.pallas_call(
        kernel,
        out_shape=out_shape,
        in_specs=in_specs,
        out_specs=out_specs,
        scratch_shapes=scratch,
        input_output_aliases=aliases,
        compiler_params=pltpu.CompilerParams(vmem_limit_bytes=10 << 20),
    )(*args)


def keep(condition, array):
    return jnp.where(condition, array, jnp.zeros_like(array))


def line_kernel(row_ref, *refs):
    _, _, x, _ = coordinates()
    line, (before_ref, plane_ref) = refs[:3], refs[3:]
    before = jnp.zeros(row_ref.shape, jnp.float32)
    for k in range(1, 4):
        before = before + keep((x ^ k) < x, line[k - 1][...])
    before_ref[...] = before
    plane_ref[...] = (row_ref[...] + line[0][...]) + (line[1][...] + line[2][...])


def prefix_kernel(before_ref, plane_ref, other_ref, *refs):
    z, core, x, y = coordinates()
    column, ring, sums = refs[:3], refs[3:7], refs[7:11]
    rows_before = before_ref[...] + keep(core == 1, other_ref[...])
    for k in range(1, 4):
        rows_before = rows_before + keep((z ^ k) < z, column[k - 1][...])
    states = [r[...] for r in ring]
    head = core * 4 + x
    for j in range(4):
        shorter = rows_before
        for k in range(4):
            if k != j:
                shorter = shorter + keep((y ^ k) < (y ^ j), states[k])
        sums[j][:STATE_ROWS] = shorter
        share = pl.multiple_of(head // 2 * DK + (y ^ j) * SHARE_ROWS, SHARE_ROWS)
        rows = pl.ds(share, SHARE_ROWS)
        chip = plane_ref[rows] + other_ref[rows]
        sums[j][STATE_ROWS:] = chip + (column[0][rows] + column[1][rows] + column[2][rows])


def small_call(kernel, out_shapes, *args):
    return pl.pallas_call(
        kernel,
        out_shape=[jax.ShapeDtypeStruct(s, jnp.float32) for s in out_shapes],
        in_specs=[IN_VMEM] * len(args),
        out_specs=[IN_VMEM] * len(out_shapes),
        compiler_params=pltpu.CompilerParams(vmem_limit_bytes=4 << 20),
    )(*args)


def steps(queries, key_rows, value_rows, norm_gain):
    total, keys, values = totals(key_rows, value_rows)
    atts, befores = [], []
    for g in range(GROUPS):
        attended, before, *fetched = inside(g, queries, keys, values)
        if g == 0:
            queries = fetched[0]
        atts.append(attended)
        befores.append(before)

    ring = [total[0]] + [exchange(total[k], dy=k) for k in range(1, 4)]
    row_sum = (ring[0] + ring[1]) + (ring[2] + ring[3])
    line = [exchange(row_sum, dx=k) for k in range(1, 4)]
    group = (STATE_ROWS, LANES)
    before, plane = small_call(line_kernel, [group, group], row_sum, *line)
    other = exchange(plane, dc=1)
    chip_sum = plane + other
    column = [exchange(chip_sum, dz=k) for k in range(1, 4)]
    sums = small_call(
        prefix_kernel, [(STATE_ROWS + SHARE_ROWS, LANES)] * 4, before, plane, other, *column, *ring
    )
    prefixes = [sums[0]] + [exchange(sums[k], dy=k) for k in TURNS[1:]]
    gain = norm_gain.reshape(1, WIDTH)
    stages, mixed = [], None
    for g in range(GROUPS):
        result = output(
            g, atts[g], befores[g], queries, gain, prefixes, stages, mixed
        )
        stages.append(result[-1])
        if g == 1:
            mixed = result[0]
    return (result[0], result[1].reshape(8 * LANES))


def solution(mesh):
    return jax.shard_map(
        steps,
        mesh=mesh,
        in_specs=(P(AXES, None), P(AXES, None), P(AXES, None), P()),
        out_specs=(P(AXES, None), P(AXES)),
        check_vma=False,
    )
```
